32 devices in a mesh: grp: 2 (over core), blk: 16 (over z, y, x).
Axes of the slice: x: 2, y: 2, z: 4, core: 2. Of those that a mesh axis runs over, the one named last changes fastest.
Arguments:
- ints: bfloat16 [16, 1536, 4096], P('blk', 'grp'), may hold values from -0.375 to 0.375
- occ_energy: float32 [400], replicated, may hold values from -2 to -0.3
- occ_window: int32 [16], replicated, may hold values from 0 to 399, as said below
- virt_energy: float32 [1536], replicated, may hold values from 0.3 to 3
Outputs:
- virt_density: float32 [1536, 768], P(('grp', 'blk'))
- pair_energy: float32 [16, 4], P('blk')
The draws below stay inside these ranges and needn't reach their ends.
Inputs may be any that keep to these rules, and one draw needn't show every extreme that they name: `occ_window`: distinct indices into occ_energy.
All inputs are finite; a program needn't handle non-finite values.
Results may differ from the reference program's by a relative error of at most 0.0003.
Values may be sent and summed in bfloat16 or wider, within the bound.
A program may use at most 64 MiB of HBM per device.

```python
import jax
import jax.numpy as jnp
from jax import lax

NVIRT = 1536
NAUX = 4096
NOCC_ALL = 400
OCC_DEV = 1
STEPS = 4
NOCC = 16
N_GRP = 2
N_BLK = 16


def draw_occ_window(key, part):
    return jax.random.permutation(key, NOCC_ALL)[:NOCC].astype(jnp.int32)


def spiked(array, rng, source, target, parts, factor):
    owner, partner = [(jnp.arange(array.shape[axis_at]) // (array.shape[axis_at] // parts)).reshape([-1 if axis == axis_at else 1 for axis in range(array.ndim)]) for axis_at in (source, target)]
    chosen = jax.random.permutation(rng, parts)[partner]
    strong = (owner == chosen) | (owner == (partner + parts // 2) % parts)
    return jnp.where(strong, factor * array, array)


def steps_of(stream_key, dims, split, least, largest):
    gain, own = 1.0, jax.random.fold_in(stream_key, 6)
    for position, shards_of in split:
        steps = jnp.exp(jax.random.uniform(jax.random.fold_in(own, position), (shards_of,), jnp.float32, least / len(split), largest / len(split)))
        gain = gain * jnp.repeat(steps, dims[position] // shards_of).reshape([-1 if axis == position else 1 for axis in range(len(dims))])
    return gain


def bell_draw_with(stream_key, dims, scale, reach, shards, heavy, kind=jnp.bfloat16):
    drawn = scale * jax.random.normal(stream_key, dims, jnp.float32)
    if shards:
        drawn = drawn * steps_of(stream_key, dims, shards, -0.22, 0.18)
    return jnp.clip(spiked(drawn, jax.random.fold_in(stream_key, 3), *heavy), -reach, reach).astype(kind)


def setup_inputs(seed: int = 0) -> dict:
    keys = jax.random.split(jax.random.key(seed), 5)
    ints = bell_draw_with(keys[0], (NOCC, NVIRT, NAUX), (0.5 * NAUX ** -0.25), 0.375, ((0, 16), (1, 2)), (0, 1, 16, 2.0))
    occ_energy = jnp.clip(jax.random.uniform(keys[1], (NOCC_ALL,), jnp.float32, -2.0, -0.3), -2.0, -0.3)
    occ_window = draw_occ_window(jax.random.fold_in(keys[4], 71), 0)
    virt_energy = jnp.clip(jax.random.uniform(keys[3], (NVIRT,), jnp.float32, 0.3, 3.0), 0.3, 3.0)
    return {"ints": ints, "occ_energy": occ_energy, "occ_window": occ_window, "virt_energy": virt_energy}


def reference(ints, occ_energy, occ_window, virt_energy):
    occ_levels = occ_energy[occ_window]
    block_size = NVIRT // N_GRP
    pair_blocks = N_GRP // 2
    virt_pairs = virt_energy.reshape(pair_blocks, 2 * block_size)
    window_pos = jnp.arange(NOCC, dtype=jnp.int32)
    density = jnp.zeros((NVIRT, block_size), jnp.float32)
    energy_list = []
    for cycle_step in range(STEPS):
        for within in range(OCC_DEV):
            partner_idx = (((window_pos // OCC_DEV - cycle_step) % N_BLK) * OCC_DEV + within).astype(jnp.int32)
            occ_partner = occ_levels[partner_idx]

            def single_pair(inputs_in):
                row_ints, partner_at, occ_row, occ_col = inputs_in
                col_ints = lax.dynamic_index_in_dim(ints, partner_at, 0, keepdims=False)
                left = row_ints.astype(jnp.float32).reshape(pair_blocks, 2 * block_size, NAUX)
                right = col_ints.astype(jnp.float32).reshape(pair_blocks, 2 * block_size, NAUX)
                coupling = jnp.einsum('qap,qbp->qab', left, right, precision=lax.Precision.HIGHEST)
                denominator = virt_pairs[:, :, None] + virt_pairs[:, None, :] - occ_row - occ_col
                amplitude = coupling / denominator
                product = jnp.einsum('qab,qcb->qac', amplitude, amplitude, precision=lax.Precision.HIGHEST)
                blocks = jnp.stack([product[:, :block_size, :block_size], product[:, block_size:, block_size:]], 1)
                pair_value = -jnp.sum(amplitude * coupling) / (block_size * block_size)
                return blocks.reshape(NVIRT, block_size), pair_value

            blocks, values = lax.map(single_pair, (ints, partner_idx, occ_levels, occ_partner))
            density = density + jnp.sum(blocks, axis=0)
            energy_list.append(values)
    return density / (NOCC * STEPS * OCC_DEV), jnp.stack(energy_list, axis=1)
```

```python
import jax
import jax.numpy as jnp
from jax import lax
from jax.sharding import PartitionSpec as P

STEPS = 4
CHUNKS = 1
RELAY = False


def from_partner(block, axis, stride):
    count = lax.axis_size(axis)
    route = []
    for low in range(count):
        high = low | 1 << stride
        if high != low and high < count:
            route += [(low, high), (high, low)]
    return lax.ppermute(block, axis, route)


def shifted(shard, axis, by):
    peers = lax.axis_size(axis)
    return lax.ppermute(shard, axis, [(i, (i + by) % peers) for i in range(peers)])


def lookup_many(values_in, where_at):
    positions = jnp.arange(values_in.shape[0], dtype=jnp.int32)
    matches = positions[None, :] == where_at[:, None]
    return jnp.sum(
        jnp.where(matches, values_in[None, :], jnp.zeros_like(values_in)[None, :]), axis=1
    )


def fetched(pieces, block_index, block_count):
    if not RELAY or block_count % 4:
        return (
            [shifted(piece, "blk", -2) for piece in pieces],
            [shifted(piece, "blk", 1) for piece in pieces],
        )
    blocks = range(block_count)
    cross_y = [(c, c ^ 2) for c in blocks]
    down = [(c, (c - 4) % block_count) for c in blocks if c & 2]
    evens = [(c, c + 1) for c in blocks if c % 2 == 0]
    odds = [(c, (c + (-1 if c & 2 else 3)) % block_count) for c in blocks if c % 2]
    upper = (block_index & 2) != 0
    odd = (block_index & 1) != 0
    further, back = [], []
    for piece in pieces:
        over = lax.ppermute(piece, "blk", cross_y)
        direct = lax.ppermute(piece, "blk", evens)
        relayed = lax.ppermute(over, "blk", odds)
        further.append(jnp.where(upper, lax.ppermute(over, "blk", down), over))
        back.append(jnp.where(odd, direct, relayed))
    return further, back


def local(ints, occ_energy, occ_window, virt_energy):
    occ_dev = ints.shape[0]
    virt_width = ints.shape[1]
    occ_count = occ_window.shape[0]
    block_count = occ_count // occ_dev
    group_index = lax.axis_index("grp")
    block_index = lax.axis_index("blk")
    mirror_index = group_index + 1 - 2 * (group_index % 2)
    virt_own = lax.dynamic_slice_in_dim(virt_energy, group_index * virt_width, virt_width)
    virt_mirror = lax.dynamic_slice_in_dim(virt_energy, mirror_index * virt_width, virt_width)
    local_rows = jnp.arange(occ_dev, dtype=jnp.int32)

    def levels(offset):
        block = (block_index + offset) % block_count
        return lookup_many(occ_energy, lookup_many(occ_window, block * occ_dev + local_rows))

    occ_own, occ_back, occ_further = levels(0), levels(-1), levels(2)
    chunks = CHUNKS if virt_width % (16 * CHUNKS) == 0 else 1
    size = virt_width // chunks
    pieces = [ints[:, n * size : (n + 1) * size] for n in range(chunks)]
    mirror = from_partner(ints, "grp", 0)
    further_pieces, back_pieces = fetched(pieces, block_index, block_count)
    virt_pieces = [
        (virt_own[n * size : (n + 1) * size], virt_mirror[n * size : (n + 1) * size])
        for n in range(chunks)
    ]

    def tile(rows, cols, virt_cols, occ_rows, occ_cols):
        coupling = jnp.einsum("rap,tbp->rtab", rows, cols, preferred_element_type=jnp.float32)
        denominator = (
            virt_own[None, None, :, None]
            + virt_cols[None, None, None, :]
            - occ_rows[:, None, None, None]
            - occ_cols[None, :, None, None]
        )
        amplitude = coupling / denominator
        square = amplitude * amplitude
        energy = -jnp.sum(square * denominator, axis=(2, 3)) / (virt_width * virt_width)
        kept = lax.reduce_precision(amplitude, exponent_bits=8, mantissa_bits=7)
        high = kept.astype(jnp.bfloat16)
        low = (amplitude - kept).astype(jnp.bfloat16)
        main = jnp.einsum("rtab,rtcb->ac", high, high, preferred_element_type=jnp.float32)
        side = jnp.einsum("rtab,rtcb->ac", high, low, preferred_element_type=jnp.float32)
        return main, side, energy

    def add(one, other):
        return tuple(a + b for a, b in zip(one, other))

    zero = add(
        tile(ints, ints, virt_own, occ_own, occ_own),
        tile(ints, mirror, virt_mirror, occ_own, occ_own),
    )
    one = None
    for piece, (near, far) in zip(back_pieces, virt_pieces):
        part = add(
            tile(ints, piece, near, occ_own, occ_back),
            tile(ints, from_partner(piece, "grp", 0), far, occ_own, occ_back),
        )
        one = part if one is None else add(one, part)
    further = jnp.concatenate(further_pieces, axis=1)
    two = add(
        tile(further, ints, virt_own, occ_further, occ_own),
        tile(further, mirror, virt_mirror, occ_further, occ_own),
    )
    three = None
    for piece, (near, far) in zip(back_pieces, virt_pieces):
        part = add(
            tile(further, piece, near, occ_further, occ_back),
            tile(further, from_partner(piece, "grp", 0), far, occ_further, occ_back),
        )
        three = part if three is None else add(three, part)
    main, side = add(add(zero[:2], one[:2]), add(two[:2], three[:2]))
    density = main + side + side.T
    shares = lax.psum_scatter(density, "blk", scatter_dimension=0, tiled=True) / (
        occ_count * STEPS * occ_dev
    )
    sent = shifted(jnp.concatenate([two[2], three[2]], axis=1), "blk", 2)
    energies = jnp.concatenate([zero[2], one[2], sent], axis=1)
    return (shares, energies + from_partner(energies, "grp", 0))


def solution(mesh):
    return jax.shard_map(
        local,
        mesh=mesh,
        in_specs=(P("blk", "grp", None), P(), P(), P()),
        out_specs=(P(("grp", "blk"), None), P("blk", None)),
        check_vma=False,
    )
```
